32 devices in a mesh: blk: 8 (over z, core), uly: 4 (over y, x).
Axes of the slice: x: 2, y: 2, z: 4, core: 2. Of those that a mesh axis runs over, the one named last changes fastest.
Arguments:
- queries: bfloat16 [1024, 128, 128], P(('blk', 'uly')), may hold values from -8 to 8
- query_tangents: bfloat16 [1024, 128, 4, 128], P(('blk', 'uly')), may hold values from -6 to 6
- keys: bfloat16 [1024, 8, 128], P(('blk', 'uly')), may hold values from -8 to 8
- key_tangents: bfloat16 [1024, 8, 4, 128], P(('blk', 'uly')), may hold values from -6 to 6
- values: bfloat16 [1024, 8, 128], P(('blk', 'uly')), may hold values from -6 to 6
- value_tangents: bfloat16 [1024, 8, 4, 128], P(('blk', 'uly')), may hold values from -6 to 6
- span_order: int32 [16], replicated, may hold values from 0 to 15, as said below
Outputs:
- attention_out: bfloat16 [1024, 128, 128], P(('blk', 'uly'))
- tangent_out: bfloat16 [1024, 128, 4, 128], P(('blk', 'uly'))
The draws below stay inside these ranges and needn't reach their ends.
Inputs may be any that keep to these rules, and one draw needn't show every extreme that they name: span_order is a permutation of the span positions; for every b the stored spans 2 * b and 2 * b + 1 hold positions c and 15 - c for some c.
All inputs are finite; a program needn't handle non-finite values.
Results may differ from the reference program's by a relative error of at most 0.0055.
Values may be sent and summed in bfloat16 or wider, within the bound.
A program may use at most 128 MiB of HBM per device.

```python
import jax
import jax.numpy as jnp
from jax import lax

HD = 128
HQ = 128
KVH = 8
P_SIZE = 4
SEQ_DEV = 128
SEQ = 1024
SPAN = 64
SPANS = 16


def drawn_pair(key):
    query_key = jax.random.fold_in(key, 11)
    keys_key = jax.random.fold_in(key, 12)
    queries = jax.random.truncated_normal(query_key, -4.0, 4.0, (SEQ, HQ, HD), jnp.float32)
    keyset = jax.random.truncated_normal(keys_key, -4.0, 4.0, (SEQ, KVH, HD), jnp.float32)
    return (queries, keyset)


def draw_queries(key, part):
    return drawn_pair(key)[0].astype(jnp.bfloat16)


def draw_keys(key, part):
    return drawn_pair(key)[1].astype(jnp.bfloat16)


def draw_span_order(key, part):
    pairs = SPANS // 2
    chosen = jax.random.permutation(jax.random.fold_in(key, 21), pairs).astype(jnp.int32)
    flipped = jax.random.randint(jax.random.fold_in(key, 22), (pairs,), 0, 2, jnp.int32)
    first = jnp.where(flipped == 1, chosen, SPANS - 1 - chosen)
    second = SPANS - 1 - first
    return jnp.stack([first, second], axis=1).reshape(SPANS).astype(jnp.int32)


def block_levels(stream_key, dims, pieces, least, high):
    factor_of, own = 1.0, jax.random.fold_in(stream_key, 6)
    for dim, blocks in pieces:
        heights = jnp.exp(jax.random.uniform(jax.random.fold_in(own, dim), (blocks,), jnp.float32, least / len(pieces), high / len(pieces)))
        factor_of = factor_of * jnp.repeat(heights, dims[dim] // blocks).reshape([-1 if axis == dim else 1 for axis in range(len(dims))])
    return factor_of


def bell_draw(stream_key, extent, deviation, limit, shards=(), kind=jnp.bfloat16):
    drawn = deviation * jax.random.normal(stream_key, extent, jnp.float32)
    if shards:
        drawn = drawn * block_levels(stream_key, extent, shards, -0.22, 0.18)
    return jnp.clip(drawn, -limit, limit).astype(kind)


def setup_inputs(seed: int = 0) -> dict:
    key_of = jax.random.split(jax.random.key(seed), 8)
    return {
        "queries": draw_queries(jax.random.fold_in(key_of[7], 71), 0),
        "query_tangents": bell_draw(key_of[1], (SEQ, HQ, P_SIZE, HD), 1.0, 6.0, ((0, 32),)),
        "keys": draw_keys(jax.random.fold_in(key_of[7], 71), 0),
        "key_tangents": bell_draw(key_of[3], (SEQ, KVH, P_SIZE, HD), 1.0, 6.0, ((0, 32),)),
        "values": bell_draw(key_of[4], (SEQ, KVH, HD), 1.0, 6.0, ((0, 32),)),
        "value_tangents": bell_draw(key_of[5], (SEQ, KVH, P_SIZE, HD), 1.0, 6.0, ((0, 32),)),
        "span_order": draw_span_order(jax.random.fold_in(key_of[7], 71), 0),
    }


def reference(queries, query_tangents, keys, key_tangents, values, value_tangents, span_order):
    stored = jnp.arange(SEQ, dtype=jnp.int32)
    position = (span_order[stored // SPAN] * SPAN + stored % SPAN).astype(jnp.int32)
    scaling = HD ** -0.5
    group = HQ // KVH
    block_rows = SEQ_DEV
    block_total = SEQ // block_rows
    keys_wide = keys.astype(jnp.float32)
    key_tan_wide = key_tangents.astype(jnp.float32)
    values_wide = values.astype(jnp.float32)
    value_tan_wide = value_tangents.astype(jnp.float32)
    highest = lax.Precision.HIGHEST

    def one_block(index):
        head = (index // block_total).astype(jnp.int32)
        kv_head = (head // group).astype(jnp.int32)
        begin = ((index % block_total) * block_rows).astype(jnp.int32)
        zero = jnp.zeros((), jnp.int32)
        query_block = lax.dynamic_slice(queries, (begin, head, zero), (block_rows, 1, HD))[:, 0]
        tangent_block = lax.dynamic_slice(query_tangents, (begin, head, zero, zero), (block_rows, 1, P_SIZE, HD))[:, 0]
        key_half = lax.dynamic_index_in_dim(keys, kv_head, 1, keepdims=False)
        value_half = lax.dynamic_index_in_dim(values, kv_head, 1, keepdims=False)
        key_f = lax.dynamic_index_in_dim(keys_wide, kv_head, 1, keepdims=False)
        key_tan_f = lax.dynamic_index_in_dim(key_tan_wide, kv_head, 1, keepdims=False)
        value_f = lax.dynamic_index_in_dim(values_wide, kv_head, 1, keepdims=False)
        value_tan_f = lax.dynamic_index_in_dim(value_tan_wide, kv_head, 1, keepdims=False)
        query_places = lax.dynamic_slice_in_dim(position, begin, block_rows)
        scores = jnp.dot(query_block, key_half.T, preferred_element_type=jnp.float32) * scaling
        visible = position[None, :] <= query_places[:, None]
        scores = jnp.where(visible, scores, -1e30)
        top = jnp.max(scores, axis=1, keepdims=True)
        weights_full = jnp.where(visible, jnp.exp(scores - top), 0.0)
        total = jnp.sum(weights_full, axis=1)
        weights = weights_full.astype(jnp.bfloat16)
        score_tan = jnp.einsum("qpd,kd->pqk", tangent_block.astype(jnp.float32), key_f, precision=highest)
        score_tan = score_tan + jnp.einsum("qd,kpd->pqk", query_block.astype(jnp.float32), key_tan_f, precision=highest)
        score_tan = score_tan * scaling
        weighted = weights_full[None] * score_tan
        shift = jnp.sum(weighted, axis=2)
        weighted_half = weighted.astype(jnp.bfloat16)
        primal_sum = jnp.dot(weights, value_half, preferred_element_type=jnp.float32)
        tangent_sum = jnp.einsum("pqk,kd->pqd", weighted_half.astype(jnp.float32), value_f, precision=highest)
        tangent_sum = tangent_sum + jnp.einsum("qk,kpd->pqd", weights.astype(jnp.float32), value_tan_f, precision=highest)
        primal = primal_sum / total[:, None]
        tangent = tangent_sum / total[None, :, None] - primal[None] * (shift / total[None])[..., None]
        return primal.astype(jnp.bfloat16), tangent.astype(jnp.bfloat16)

    outputs, tangents = lax.map(one_block, jnp.arange(HQ * block_total, dtype=jnp.int32))
    outputs = outputs.reshape(HQ, block_total, block_rows, HD).transpose(1, 2, 0, 3).reshape(SEQ, HQ, HD)
    tangents = tangents.reshape(HQ, block_total, P_SIZE, block_rows, HD).transpose(1, 3, 0, 2, 4).reshape(SEQ, HQ, P_SIZE, HD)
    return outputs, tangents
```

```python
import functools

import jax
import jax.numpy as jnp
from jax import lax
from jax.experimental import pallas as pl
from jax.experimental.pallas import tpu as pltpu
from jax.sharding import PartitionSpec as P

TILE_SCORES = 256 * 1024


def positions(stored, span_order, span_rows):
    span_ids = stored // span_rows
    table_ids = jnp.arange(span_order.shape[0], dtype=jnp.int32)
    looked_up = jnp.sum(
        jnp.where(span_ids[:, None] == table_ids[None, :], span_order[None, :], 0), axis=1
    )
    return looked_up * span_rows + stored % span_rows


def exchange_and_attend(
    sizes, probes, group, packed, q_hbm, qt_hbm, bias_hbm, out_ref, tan_ref, *scratch
):
    gathered, q_ref, qt_ref, bias_ref, wide_in, wide_out, local_sem = scratch[:7]
    z_send, z_recv, one_send, one_recv, many_send, many_recv = scratch[7:]
    depth, side_y, side_x = sizes
    kv_heads = packed.shape[0]
    rows, _, head_size = q_ref.shape
    all_rows = rows * group
    keys_total = bias_ref.shape[1]
    tile = min(all_rows, TILE_SCORES // keys_total)
    scaling = head_size ** (-0.5)
    blk, uly = lax.axis_index("blk"), lax.axis_index("uly")
    z, c = blk // 2, blk % 2
    y, x = uly // side_x, uly % side_x

    def remote(src, dst, send, recv, target):
        return pltpu.make_async_remote_copy(
            src_ref=src,
            dst_ref=dst,
            send_sem=send,
            recv_sem=recv,
            device_id=target,
            device_id_type=pl.DeviceIdType.MESH,
        )

    def at_z(d):
        return (((z + d) % depth) * 2 + c, uly)

    def at_y(d):
        return (blk, ((y + d) % side_y) * side_x + x)

    at_x = (blk, y * side_x + (1 - x))
    at_core = (z * 2 + (1 - c), uly)

    def send_z(h):
        return [
            remote(
                packed.at[h],
                gathered.at[h, :, c, y, x, z],
                z_send.at[h, d - 1],
                z_recv.at[h, d - 1],
                at_z(d),
            )
            for d in range(1, depth)
        ]

    def to_x(h, which, block):
        return [remote(block, block, one_send.at[h, which], one_recv.at[h, which], at_x)]

    def to_y(h, which, block):
        return [
            remote(
                block,
                block,
                many_send.at[h, which, d - 1],
                many_recv.at[h, which, d - 1],
                at_y(d),
            )
            for d in range(1, side_y)
        ]

    def second(h):
        return to_x(h, 0, gathered.at[h, 0, c, y, x]) + to_y(h, 0, gathered.at[h, 1, c, y, x])

    def third(h):
        return to_y(h, 1, gathered.at[h, 0, c, y]) + to_x(h, 1, gathered.at[h, 1, c, :, x])

    def across_chip(h):
        block = gathered.at[h, :, c]
        return [remote(block, block, one_send.at[h, 2], one_recv.at[h, 2], at_core)]

    locals_in = [
        pltpu.make_async_copy(packed, gathered.at[:, :, c, y, x, z], local_sem.at[0]),
        pltpu.make_async_copy(q_hbm, q_ref, local_sem.at[1]),
        pltpu.make_async_copy(qt_hbm, qt_ref, local_sem.at[2]),
        pltpu.make_async_copy(bias_hbm, bias_ref, local_sem.at[3]),
    ]
    for copy in locals_in:
        copy.start()
    barrier = pltpu.get_barrier_semaphore()
    partners = [at_z(d) for d in range(1, depth)] + [at_y(d) for d in range(1, side_y)]
    partners += [at_x, at_core]
    for target in partners:
        pl.semaphore_signal(
            barrier, inc=1, device_id=target, device_id_type=pl.DeviceIdType.MESH
        )
    pl.semaphore_wait(barrier, len(partners))

    @pl.loop(0, kv_heads)
    def _(h):
        for copy in send_z(h):
            copy.start()

    for copy in locals_in:
        copy.wait()

    contract_last = (((1,), (1,)), ((), ()))

    def attend(h):
        def stream(half, index):
            return gathered[h, half, :, :, :, :, index].reshape(keys_total, head_size)

        q_rows = q_ref[:, pl.ds(pl.multiple_of(h * group, group), group), :]
        query = q_rows.reshape(all_rows, head_size)
        wide = group * probes
        qt_rows = qt_ref[:, pl.ds(pl.multiple_of(h * wide, wide), wide), :]
        wide_in[...] = qt_rows.reshape(all_rows * probes, head_size).astype(jnp.float32)
        key = stream(0, 0)
        value = stream(1, 0)
        value_all = jnp.concatenate([stream(1, p) for p in range(1 + probes)], axis=1)
        for start in range(0, all_rows, tile):
            q = query[start : start + tile]
            scores = lax.dot_general(q, key, contract_last, preferred_element_type=jnp.float32)
            scores = scores * scaling + bias_ref[start : start + tile, :]
            top = jnp.max(scores, axis=1, keepdims=True)
            weights = jnp.exp(scores - top)
            inverse = 1.0 / jnp.sum(weights, axis=1, keepdims=True)
            sums = jnp.dot(
                weights.astype(jnp.bfloat16), value_all, preferred_element_type=jnp.float32
            )
            primal = sums[:, :head_size] * inverse
            scaled = weights * scaling
            for p in range(probes):
                picked = pl.ds(start * probes + p, tile, stride=probes)
                left = jnp.concatenate([wide_in[picked, :].astype(jnp.bfloat16), q], axis=1)
                right = jnp.concatenate([key, stream(0, 1 + p)], axis=1)
                score_tan = lax.dot_general(
                    left, right, contract_last, preferred_element_type=jnp.float32
                )
                weighted = scaled * score_tan
                shift = jnp.sum(weighted, axis=1, keepdims=True)
                total = sums[:, head_size * (1 + p) : head_size * (2 + p)] + jnp.dot(
                    weighted.astype(jnp.bfloat16), value, preferred_element_type=jnp.float32
                )
                wide_out[picked, :] = (total - primal * shift) * inverse
            out_ref[
                start // group : (start + tile) // group,
                pl.ds(pl.multiple_of(h * group, group), group),
                :,
            ] = primal.astype(jnp.bfloat16).reshape(tile // group, group, head_size)
        tan_ref[:, pl.ds(pl.multiple_of(h * wide, wide), wide), :] = (
            wide_out[...].astype(jnp.bfloat16).reshape(rows, wide, head_size)
        )

    @pl.loop(0, kv_heads + 3)
    def _(t):
        @pl.when(t < kv_heads)
        def _():
            for copy in send_z(t):
                copy.wait_recv()
            for copy in second(t):
                copy.start()

        @pl.when((t >= 1) & (t < kv_heads + 1))
        def _():
            for copy in second(t - 1):
                copy.wait_recv()
            for copy in third(t - 1):
                copy.start()

        @pl.when((t >= 2) & (t < kv_heads + 2))
        def _():
            for copy in third(t - 2):
                copy.wait_recv()
            for copy in across_chip(t - 2):
                copy.start()

        @pl.when(t >= 3)
        def _():
            for copy in across_chip(t - 3):
                copy.wait_recv()
            attend(t - 3)

    @pl.loop(0, kv_heads)
    def _(h):
        for copy in send_z(h) + second(h) + third(h) + across_chip(h):
            copy.wait_send()


def per_device(queries, query_tangents, keys, key_tangents, values, value_tangents, span_order):
    rows, heads, head_size = queries.shape
    kv_heads = keys.shape[1]
    probes = key_tangents.shape[2]
    group = heads // kv_heads
    blks, ulys = lax.axis_size("blk"), lax.axis_size("uly")
    depth, side_x, side_y = blks // 2, 2, ulys // 2
    total_rows = rows * blks * ulys
    span_rows = total_rows // span_order.shape[0]
    tangents = query_tangents.reshape(rows, heads * probes, head_size)
    packed = jnp.stack(
        [
            jnp.concatenate(
                [
                    jnp.transpose(primal, (1, 0, 2))[:, None],
                    jnp.transpose(tangent, (1, 2, 0, 3)),
                ],
                axis=1,
            )
            for primal, tangent in ((keys, key_tangents), (values, value_tangents))
        ],
        axis=1,
    )
    me = lax.axis_index("blk") * ulys + lax.axis_index("uly")
    own = positions(me * rows + jnp.arange(rows, dtype=jnp.int32), span_order, span_rows)
    places = positions(jnp.arange(total_rows, dtype=jnp.int32), span_order, span_rows)
    places = jnp.transpose(
        places.reshape(depth, 2, side_y, side_x, rows), (1, 2, 3, 0, 4)
    ).reshape(total_rows)
    bias = jnp.where(places[None, :] <= own[:, None], 0.0, -1e30).astype(jnp.float32)
    bias = jnp.broadcast_to(bias[:, None], (rows, group, total_rows)).reshape(
        rows * group, total_rows
    )
    wide_rows = rows * group * probes
    pairs = rows * heads * total_rows
    dma = pltpu.SemaphoreType.DMA
    attention, tangent = pl.pallas_call(
        functools.partial(exchange_and_attend, (depth, side_y, side_x), probes, group),
        in_specs=[pl.BlockSpec(memory_space=pl.ANY)] * 4,
        out_specs=[pl.BlockSpec(memory_space=pltpu.VMEM)] * 2,
        out_shape=[
            jax.ShapeDtypeStruct(queries.shape, queries.dtype),
            jax.ShapeDtypeStruct(tangents.shape, tangents.dtype),
        ],
        scratch_shapes=[
            pltpu.VMEM(
                (kv_heads, 2, 2, side_y, side_x, depth, 1 + probes, rows, head_size),
                keys.dtype,
            ),
            pltpu.VMEM(queries.shape, queries.dtype),
            pltpu.VMEM(tangents.shape, tangents.dtype),
            pltpu.VMEM(bias.shape, bias.dtype),
            pltpu.VMEM((wide_rows, head_size), jnp.float32),
            pltpu.VMEM((wide_rows, head_size), jnp.float32),
            dma((4,)),
            dma((kv_heads, depth - 1)),
            dma((kv_heads, depth - 1)),
            dma((kv_heads, 3)),
            dma((kv_heads, 3)),
            dma((kv_heads, 2, side_y - 1)),
            dma((kv_heads, 2, side_y - 1)),
        ],
        cost_estimate=pl.CostEstimate(
            flops=2 * pairs * head_size * (2 + 4 * probes),
            transcendentals=pairs,
            bytes_accessed=packed.size * 2,
        ),
        compiler_params=pltpu.CompilerParams(
            collective_id=0, has_side_effects=True, vmem_limit_bytes=67043328
        ),
    )(packed, queries, tangents, bias)
    return attention, tangent.reshape(query_tangents.shape)


def solution(mesh):
    placed = (
        P(("blk", "uly"), None, None),
        P(("blk", "uly"), None, None, None),
        P(("blk", "uly"), None, None),
        P(("blk", "uly"), None, None, None),
        P(("blk", "uly"), None, None),
        P(("blk", "uly"), None, None, None),
        P(),
    )
    return jax.shard_map(
        per_device,
        mesh=mesh,
        in_specs=placed,
        out_specs=(P(("blk", "uly"), None, None), P(("blk", "uly"), None, None, None)),
        check_vma=False,
    )
```

```python
import functools

import jax
import jax.numpy as jnp
import numpy as np
from jax import lax
from jax.experimental import pallas as pl
from jax.experimental.pallas import tpu as pltpu
from jax.sharding import PartitionSpec as P

TILE_SCORES = 256 * 1024
LAST = 2


def exchange_and_attend(
    sizes, probes, group, span_rows, order_ref, place_ref, packed, packed_last, q_hbm, qt_hbm,
    out_ref, tan_ref, *scratch
):
    pair, last, q_ref, qt_ref, places, bias_ref, wide_in, wide_out, local_sem = scratch[:9]
    z_send, z_recv, one_send, one_recv, many_send, many_recv = scratch[9:15]
    plane_send, plane_recv, step_send, step_recv = scratch[15:]
    depth, side_y, side_x = sizes
    kv_heads = packed.shape[0]
    rows, _, head_size = q_ref.shape
    all_rows = rows * group
    keys_total = bias_ref.shape[1]
    tile = min(all_rows, TILE_SCORES // keys_total)
    scaling = head_size ** (-0.5)
    blk, uly = lax.axis_index("blk"), lax.axis_index("uly")
    z, c = blk // 2, blk % 2
    y, x = uly // side_x, uly % side_x

    def remote(src, dst, send, recv, target):
        return pltpu.make_async_remote_copy(
            src_ref=src,
            dst_ref=dst,
            send_sem=send,
            recv_sem=recv,
            device_id=target,
            device_id_type=pl.DeviceIdType.MESH,
        )

    def at_z(d):
        return (((z + d) % depth) * 2 + c, uly)

    def at_plane(dy, dx):
        return (blk, ((y + dy) % side_y) * side_x + (x + dx) % side_x)

    at_core = (z * 2 + (1 - c), uly)
    offsets = [(dy, dx) for dy in range(side_y) for dx in range(side_x) if dy or dx]

    def send_z(h):
        return [
            remote(
                packed.at[h],
                pair.at[h, :, c, z, y, x],
                z_send.at[h, d - 1],
                z_recv.at[h, d - 1],
                at_z(d),
            )
            for d in range(1, depth)
        ]

    def to_x(h, which, block):
        return [
            remote(block, block, one_send.at[h, which], one_recv.at[h, which], at_plane(0, 1))
        ]

    def to_y(h, which, block):
        return [
            remote(
                block,
                block,
                many_send.at[h, which, d - 1],
                many_recv.at[h, which, d - 1],
                at_plane(d, 0),
            )
            for d in range(1, side_y)
        ]

    def second(h):
        return to_x(h, 0, pair.at[h, 0, c, :, y, x]) + to_y(h, 0, pair.at[h, 1, c, :, y, x])

    def third(h):
        return to_y(h, 1, pair.at[h, 0, c, :, y]) + to_x(h, 1, pair.at[h, 1, c, :, :, x])

    def across_chip(h):
        return [
            remote(block, block, one_send.at[h, which], one_recv.at[h, which], at_core)
            for which, block in ((2, pair.at[h, :, c]), (3, last.at[h, c]))
        ]

    planes = [
        remote(
            packed_last, last.at[:, c, z, y, x], plane_send.at[n], plane_recv.at[n], at_plane(*d)
        )
        for n, d in enumerate(offsets)
    ]

    def each_step(h, s, act):
        for way, sign in enumerate((1, -1)):
            origin = z - sign * (s - 1)
            block = last.at[h, c, jnp.clip(origin, 0, depth - 1)]
            target = jnp.clip(z + sign, 0, depth - 1)
            copy = remote(
                block,
                block,
                step_send.at[h, s - 1, way],
                step_recv.at[h, s - 1, way],
                (target * 2 + c, uly),
            )
            arrives = z - sign * s
            sends = (origin >= 0) & (origin < depth) & (z + sign >= 0) & (z + sign < depth)
            gets = (arrives >= 0) & (arrives < depth)

            @pl.when(gets if act == "wait_recv" else sends)
            def _(copy=copy):
                getattr(copy, act)()

    locals_in = [
        pltpu.make_async_copy(packed, pair.at[:, :, c, z, y, x], local_sem.at[0]),
        pltpu.make_async_copy(packed_last, last.at[:, c, z, y, x], local_sem.at[1]),
        pltpu.make_async_copy(place_ref, places, local_sem.at[2]),
        pltpu.make_async_copy(q_hbm, q_ref, local_sem.at[3]),
        pltpu.make_async_copy(qt_hbm, qt_ref, local_sem.at[4]),
    ]
    barrier = pltpu.get_barrier_semaphore()
    partners = [at_z(d) for d in range(1, depth)] + [at_plane(*d) for d in offsets] + [at_core]
    for target in partners:
        pl.semaphore_signal(
            barrier, inc=1, device_id=target, device_id_type=pl.DeviceIdType.MESH
        )
    for copy in locals_in:
        copy.start()
    pl.semaphore_wait(barrier, len(partners))
    for copy in send_z(0) + planes + send_z(1):
        copy.start()
    for copy in locals_in:
        copy.wait()

    spans = order_ref.shape[0]
    looked_up = jnp.zeros((1, keys_total), jnp.int32)
    for span in range(spans):
        looked_up = jnp.where(places[0:1, :] == span, order_ref[span], looked_up)
    key_places = looked_up * span_rows + places[1:2, :]
    first = (blk * (side_y * side_x) + uly) * rows
    base = order_ref[first // span_rows] * span_rows + first % span_rows
    row = lax.broadcasted_iota(jnp.int32, (all_rows, 1), 0)
    row = base + lax.shift_right_logical(row, jnp.full_like(row, group.bit_length() - 1))
    bias_ref[...] = jnp.where(key_places <= row, 0.0, -1e30).astype(jnp.float32)

    for copy in planes:
        copy.wait_recv()

    contract_last = (((1,), (1,)), ((), ()))

    def attend(h):
        def stream(index):
            half = pair.shape[6]
            if index < 2 * half:
                found = pair[h, index // half, :, :, :, :, index % half]
            else:
                found = last[h, :, :, :, :, index - 2 * half]
            return found.reshape(keys_total, head_size)

        q_rows = q_ref[:, pl.ds(pl.multiple_of(h * group, group), group), :]
        query = q_rows.reshape(all_rows, head_size)
        wide = group * probes
        qt_rows = qt_ref[:, pl.ds(pl.multiple_of(h * wide, wide), wide), :]
        wide_in[...] = qt_rows.reshape(all_rows * probes, head_size).astype(jnp.float32)
        key = stream(0)
        value = stream(1 + probes)
        value_all = jnp.concatenate([stream(1 + probes + p) for p in range(1 + probes)], axis=1)
        for start in range(0, all_rows, tile):
            q = query[start : start + tile]
            scores = lax.dot_general(q, key, contract_last, preferred_element_type=jnp.float32)
            scores = scores * scaling + bias_ref[start : start + tile, :]
            top = jnp.max(scores, axis=1, keepdims=True)
            weights = jnp.exp(scores - top)
            inverse = 1.0 / jnp.sum(weights, axis=1, keepdims=True)
            sums = jnp.dot(
                weights.astype(jnp.bfloat16), value_all, preferred_element_type=jnp.float32
            )
            primal = sums[:, :head_size] * inverse
            scaled = weights * scaling
            for p in range(probes):
                picked = pl.ds(start * probes + p, tile, stride=probes)
                left = jnp.concatenate([wide_in[picked, :].astype(jnp.bfloat16), q], axis=1)
                right = jnp.concatenate([key, stream(1 + p)], axis=1)
                score_tan = lax.dot_general(
                    left, right, contract_last, preferred_element_type=jnp.float32
                )
                weighted = scaled * score_tan
                shift = jnp.sum(weighted, axis=1, keepdims=True)
                total = sums[:, head_size * (1 + p) : head_size * (2 + p)] + jnp.dot(
                    weighted.astype(jnp.bfloat16), value, preferred_element_type=jnp.float32
                )
                wide_out[picked, :] = (total - primal * shift) * inverse
            out_ref[
                start // group : (start + tile) // group,
                pl.ds(pl.multiple_of(h * group, group), group),
                :,
            ] = primal.astype(jnp.bfloat16).reshape(tile // group, group, head_size)
        tan_ref[:, pl.ds(pl.multiple_of(h * wide, wide), wide), :] = (
            wide_out[...].astype(jnp.bfloat16).reshape(rows, wide, head_size)
        )

    steps = range(1, depth)

    @pl.loop(min(0, 3 - depth), kv_heads + 3)
    def _(t):
        @pl.when((t >= 0) & (t < kv_heads - 2))
        def _():
            for copy in send_z(t + 2):
                copy.start()

        @pl.when((t >= 0) & (t < kv_heads))
        def _():
            for copy in send_z(t):
                copy.wait_recv()
            for copy in second(t):
                copy.start()

        for s in steps:
            h = t - s + depth - 2

            @pl.when((h >= 0) & (h < kv_heads))
            def _(h=h, s=s):
                if s > 1:
                    each_step(h, s - 1, "wait_recv")
                each_step(h, s, "start")

        @pl.when((t == 0) | ((t >= 2) & (t < kv_heads + 1)))
        def _():
            h = jnp.maximum(t - 1, 0)
            for copy in second(h):
                copy.wait_recv()
            for copy in third(h):
                copy.start()

        @pl.when((t >= 2) & (t < kv_heads + 2))
        def _():
            for copy in third(t - 2):
                copy.wait_recv()
            each_step(t - 2, depth - 1, "wait_recv")
            for copy in across_chip(t - 2):
                copy.start()

        @pl.when(t >= 3)
        def _():
            for copy in across_chip(t - 3):
                copy.wait_recv()
            attend(t - 3)

    for copy in planes:
        copy.wait_send()

    @pl.loop(0, kv_heads)
    def _(h):
        for copy in send_z(h) + second(h) + third(h) + across_chip(h):
            copy.wait_send()
        for s in steps:
            each_step(h, s, "wait_send")


def per_device(queries, query_tangents, keys, key_tangents, values, value_tangents, span_order):
    rows, heads, head_size = queries.shape
    kv_heads = keys.shape[1]
    probes = key_tangents.shape[2]
    group = heads // kv_heads
    blks, ulys = lax.axis_size("blk"), lax.axis_size("uly")
    depth, side_x, side_y = blks // 2, 2, ulys // 2
    total_rows = rows * blks * ulys
    span_rows = total_rows // span_order.shape[0]
    tangents = query_tangents.reshape(rows, heads * probes, head_size)
    streams = jnp.concatenate(
        [
            jnp.transpose(keys, (1, 0, 2))[:, None],
            jnp.transpose(key_tangents, (1, 2, 0, 3)),
            jnp.transpose(values, (1, 0, 2))[:, None],
            jnp.transpose(value_tangents, (1, 2, 0, 3)),
        ],
        axis=1,
    )
    half = (streams.shape[1] - LAST) // 2
    packed = streams[:, : 2 * half].reshape(kv_heads, 2, half, rows, head_size)
    packed_last = streams[:, 2 * half :]
    stored = np.arange(total_rows).reshape(depth, 2, ulys, rows)
    stored = stored.transpose(1, 0, 2, 3).reshape(total_rows)
    place_table = np.stack([stored // span_rows, stored % span_rows]).astype(np.int32)
    wide_rows = rows * group * probes
    pairs = rows * heads * total_rows
    dma = pltpu.SemaphoreType.DMA
    attention, tangent = pl.pallas_call(
        functools.partial(
            exchange_and_attend, (depth, side_y, side_x), probes, group, span_rows
        ),
        in_specs=[pl.BlockSpec(memory_space=pltpu.SMEM)]
        + [pl.BlockSpec(memory_space=pl.ANY)] * 5,
        out_specs=[pl.BlockSpec(memory_space=pltpu.VMEM)] * 2,
        out_shape=[
            jax.ShapeDtypeStruct(queries.shape, queries.dtype),
            jax.ShapeDtypeStruct(tangents.shape, tangents.dtype),
        ],
        scratch_shapes=[
            pltpu.VMEM(
                (kv_heads, 2, 2, depth, side_y, side_x, half, rows, head_size), keys.dtype
            ),
            pltpu.VMEM(
                (kv_heads, 2, depth, side_y, side_x, streams.shape[1] - 2 * half, rows, head_size),
                keys.dtype,
            ),
            pltpu.VMEM(queries.shape, queries.dtype),
            pltpu.VMEM(tangents.shape, tangents.dtype),
            pltpu.VMEM(place_table.shape, jnp.int32),
            pltpu.VMEM((rows * group, total_rows), jnp.float32),
            pltpu.VMEM((wide_rows, head_size), jnp.float32),
            pltpu.VMEM((wide_rows, head_size), jnp.float32),
            dma((5,)),
            dma((kv_heads, depth - 1)),
            dma((kv_heads, depth - 1)),
            dma((kv_heads, 4)),
            dma((kv_heads, 4)),
            dma((kv_heads, 2, side_y - 1)),
            dma((kv_heads, 2, side_y - 1)),
            dma((side_y * side_x - 1,)),
            dma((side_y * side_x - 1,)),
            dma((kv_heads, depth - 1, 2)),
            dma((kv_heads, depth - 1, 2)),
        ],
        cost_estimate=pl.CostEstimate(
            flops=2 * pairs * head_size * (2 + 4 * probes),
            transcendentals=pairs,
            bytes_accessed=packed.size * 2,
        ),
        compiler_params=pltpu.CompilerParams(
            collective_id=0, has_side_effects=True, vmem_limit_bytes=67043328
        ),
    )(span_order, place_table, packed, packed_last, queries, tangents)
    return attention, tangent.reshape(query_tangents.shape)


def solution(mesh):
    placed = (
        P(("blk", "uly"), None, None),
        P(("blk", "uly"), None, None, None),
        P(("blk", "uly"), None, None),
        P(("blk", "uly"), None, None, None),
        P(("blk", "uly"), None, None),
        P(("blk", "uly"), None, None, None),
        P(),
    )
    return jax.shard_map(
        per_device,
        mesh=mesh,
        in_specs=placed,
        out_specs=(P(("blk", "uly"), None, None), P(("blk", "uly"), None, None, None)),
        check_vma=False,
    )
```

```python
import functools

import jax
import jax.numpy as jnp
import numpy as np
from jax import lax
from jax.experimental import pallas as pl
from jax.experimental.pallas import tpu as pltpu
from jax.sharding import PartitionSpec as P

TILE_SCORES = 256 * 1024
LAST = 2


def exchange_and_attend(
    sizes, probes, group, span_rows, order_ref, place_ref, packed, packed_last, q_hbm, qt_hbm,
    out_hbm, tan_hbm, *scratch
):
    pair, last, q_ref, qt_ref, places, bias_ref, wide_in, wide_out, local_sem = scratch[:9]
    z_send, z_recv, one_send, one_recv, many_send, many_recv = scratch[9:15]
    plane_send, plane_recv, step_send, step_recv, out_ref, tan_ref, out_sem = scratch[15:]
    depth, side_y, side_x = sizes
    kv_heads = packed.shape[0]
    rows, _, head_size = q_ref.shape
    all_rows = rows * group
    keys_total = bias_ref.shape[1]
    tile = min(all_rows, TILE_SCORES // keys_total)
    scaling = head_size ** (-0.5)
    blk, uly = lax.axis_index("blk"), lax.axis_index("uly")
    z, c = blk // 2, blk % 2
    y, x = uly // side_x, uly % side_x

    def remote(src, dst, send, recv, target):
        return pltpu.make_async_remote_copy(
            src_ref=src,
            dst_ref=dst,
            send_sem=send,
            recv_sem=recv,
            device_id=target,
            device_id_type=pl.DeviceIdType.MESH,
        )

    def at_z(d):
        return (((z + d) % depth) * 2 + c, uly)

    def at_plane(dy, dx):
        return (blk, ((y + dy) % side_y) * side_x + (x + dx) % side_x)

    at_core = (z * 2 + (1 - c), uly)
    offsets = [(dy, dx) for dy in range(side_y) for dx in range(side_x) if dy or dx]

    def send_z(h):
        return [
            remote(
                packed.at[h],
                pair.at[h, :, c, z, y, x],
                z_send.at[h, d - 1],
                z_recv.at[h, d - 1],
                at_z(d),
            )
            for d in range(1, depth)
        ]

    def to_x(h, which, block):
        return [
            remote(block, block, one_send.at[h, which], one_recv.at[h, which], at_plane(0, 1))
        ]

    def to_y(h, which, block):
        return [
            remote(
                block,
                block,
                many_send.at[h, which, d - 1],
                many_recv.at[h, which, d - 1],
                at_plane(d, 0),
            )
            for d in range(1, side_y)
        ]

    def second(h):
        return to_x(h, 0, pair.at[h, 0, c, :, y, x]) + to_y(h, 0, pair.at[h, 1, c, :, y, x])

    def third(h):
        return to_y(h, 1, pair.at[h, 0, c, :, y]) + to_x(h, 1, pair.at[h, 1, c, :, :, x])

    def across_chip(h):
        return [
            remote(block, block, one_send.at[h, which], one_recv.at[h, which], at_core)
            for which, block in ((2, pair.at[h, :, c]), (3, last.at[h, c]))
        ]

    planes = [
        remote(
            packed_last, last.at[:, c, z, y, x], plane_send.at[n], plane_recv.at[n], at_plane(*d)
        )
        for n, d in enumerate(offsets)
    ]

    def each_step(h, s, act):
        for way, sign in enumerate((1, -1)):
            origin = z - sign * (s - 1)
            block = last.at[h, c, jnp.clip(origin, 0, depth - 1)]
            target = jnp.clip(z + sign, 0, depth - 1)
            copy = remote(
                block,
                block,
                step_send.at[h, s - 1, way],
                step_recv.at[h, s - 1, way],
                (target * 2 + c, uly),
            )
            arrives = z - sign * s
            sends = (origin >= 0) & (origin < depth) & (z + sign >= 0) & (z + sign < depth)
            gets = (arrives >= 0) & (arrives < depth)

            @pl.when(gets if act == "wait_recv" else sends)
            def _(copy=copy):
                getattr(copy, act)()

    locals_in = [
        pltpu.make_async_copy(packed, pair.at[:, :, c, z, y, x], local_sem.at[0]),
        pltpu.make_async_copy(packed_last, last.at[:, c, z, y, x], local_sem.at[1]),
        pltpu.make_async_copy(place_ref, places, local_sem.at[2]),
        pltpu.make_async_copy(q_hbm, q_ref, local_sem.at[3]),
        pltpu.make_async_copy(qt_hbm, qt_ref, local_sem.at[4]),
    ]
    barrier = pltpu.get_barrier_semaphore()
    partners = [at_z(d) for d in range(1, depth)] + [at_plane(*d) for d in offsets] + [at_core]
    for target in partners:
        pl.semaphore_signal(
            barrier, inc=1, device_id=target, device_id_type=pl.DeviceIdType.MESH
        )
    for copy in locals_in:
        copy.start()
    pl.semaphore_wait(barrier, len(partners))
    for copy in send_z(0) + planes + send_z(1):
        copy.start()
    for copy in locals_in:
        copy.wait()

    spans = order_ref.shape[0]
    looked_up = jnp.zeros((1, keys_total), jnp.int32)
    for span in range(spans):
        looked_up = jnp.where(places[0:1, :] == span, order_ref[span], looked_up)
    key_places = looked_up * span_rows + places[1:2, :]
    first = (blk * (side_y * side_x) + uly) * rows
    base = order_ref[first // span_rows] * span_rows + first % span_rows
    row = lax.broadcasted_iota(jnp.int32, (all_rows, 1), 0)
    row = base + lax.shift_right_logical(row, jnp.full_like(row, group.bit_length() - 1))
    bias_ref[...] = jnp.where(key_places <= row, 0.0, -1e30).astype(jnp.float32)

    for copy in planes:
        copy.wait_recv()

    contract_last = (((1,), (1,)), ((), ()))

    def attend(h):
        def stream(index):
            half = pair.shape[6]
            if index < 2 * half:
                found = pair[h, index // half, :, :, :, :, index % half]
            else:
                found = last[h, :, :, :, :, index - 2 * half]
            return found.reshape(keys_total, head_size)

        q_rows = q_ref[:, pl.ds(pl.multiple_of(h * group, group), group), :]
        query = q_rows.reshape(all_rows, head_size)
        wide = group * probes
        qt_rows = qt_ref[:, pl.ds(pl.multiple_of(h * wide, wide), wide), :]
        wide_in[...] = qt_rows.reshape(all_rows * probes, head_size).astype(jnp.float32)
        key = stream(0)
        value = stream(1 + probes)
        value_all = jnp.concatenate([stream(1 + probes + p) for p in range(1 + probes)], axis=1)
        for start in range(0, all_rows, tile):
            q = query[start : start + tile]
            scores = lax.dot_general(q, key, contract_last, preferred_element_type=jnp.float32)
            scores = scores * scaling + bias_ref[start : start + tile, :]
            top = jnp.max(scores, axis=1, keepdims=True)
            weights = jnp.exp(scores - top)
            inverse = 1.0 / jnp.sum(weights, axis=1, keepdims=True)
            sums = jnp.dot(
                weights.astype(jnp.bfloat16), value_all, preferred_element_type=jnp.float32
            )
            primal = sums[:, :head_size] * inverse
            scaled = weights * scaling
            for p in range(probes):
                picked = pl.ds(start * probes + p, tile, stride=probes)
                left = jnp.concatenate([wide_in[picked, :].astype(jnp.bfloat16), q], axis=1)
                right = jnp.concatenate([key, stream(1 + p)], axis=1)
                score_tan = lax.dot_general(
                    left, right, contract_last, preferred_element_type=jnp.float32
                )
                weighted = scaled * score_tan
                shift = jnp.sum(weighted, axis=1, keepdims=True)
                total = sums[:, head_size * (1 + p) : head_size * (2 + p)] + jnp.dot(
                    weighted.astype(jnp.bfloat16), value, preferred_element_type=jnp.float32
                )
                wide_out[picked, :] = (total - primal * shift) * inverse
            out_ref[
                start // group : (start + tile) // group,
                pl.ds(pl.multiple_of(h * group, group), group),
                :,
            ] = primal.astype(jnp.bfloat16).reshape(tile // group, group, head_size)
        tan_ref[:, pl.ds(pl.multiple_of(h * wide, wide), wide), :] = (
            wide_out[...].astype(jnp.bfloat16).reshape(rows, wide, head_size)
        )

    def put_out(h):
        wide = group * probes
        narrow_part = pl.ds(pl.multiple_of(h * group, group), group)
        wide_part = pl.ds(pl.multiple_of(h * wide, wide), wide)
        return [
            pltpu.make_async_copy(
                out_ref.at[:, narrow_part], out_hbm.at[:, narrow_part], out_sem.at[h, 0]
            ),
            pltpu.make_async_copy(
                tan_ref.at[:, wide_part], tan_hbm.at[:, wide_part], out_sem.at[h, 1]
            ),
        ]

    steps = range(1, depth)

    @pl.loop(min(0, 3 - depth), kv_heads + 3)
    def _(t):
        @pl.when((t >= 0) & (t < kv_heads))
        def _():
            for copy in send_z(t):
                copy.wait_recv()
            for copy in second(t):
                copy.start()

        @pl.when((t == 0) | ((t >= 2) & (t < kv_heads + 1)))
        def _():
            h = jnp.maximum(t - 1, 0)
            for copy in second(h):
                copy.wait_recv()
            for copy in third(h):
                copy.start()

        for s in steps:
            h = t - s + depth - 2

            @pl.when((h >= 0) & (h < kv_heads))
            def _(h=h, s=s):
                if s > 1:
                    each_step(h, s - 1, "wait_recv")
                each_step(h, s, "start")

        @pl.when((t >= 0) & (t < kv_heads - 2))
        def _():
            for copy in send_z(t + 2):
                copy.start()

        @pl.when((t >= 2) & (t < kv_heads + 2))
        def _():
            for copy in third(t - 2):
                copy.wait_recv()
            each_step(t - 2, depth - 1, "wait_recv")
            for copy in across_chip(t - 2):
                copy.start()

        @pl.when(t >= 3)
        def _():
            for copy in across_chip(t - 3):
                copy.wait_recv()
            attend(t - 3)
            for copy in put_out(t - 3):
                copy.start()

    for copy in planes:
        copy.wait_send()

    @pl.loop(0, kv_heads)
    def _(h):
        for copy in send_z(h) + second(h) + third(h) + across_chip(h):
            copy.wait_send()
        for s in steps:
            each_step(h, s, "wait_send")
        for copy in put_out(h):
            copy.wait()


def settle(parts, *refs):
    count = len(refs) // 4
    sources, targets, held, sems = (refs[n * count : (n + 1) * count] for n in range(4))

    def pieces(sources, targets, side):
        return [
            pltpu.make_async_copy(
                source.at[n * (source.shape[0] // parts) : (n + 1) * (source.shape[0] // parts)],
                target.at[n * (source.shape[0] // parts) : (n + 1) * (source.shape[0] // parts)],
                sem.at[side, n],
            )
            for n in range(parts)
            for source, target, sem in zip(sources, targets, sems)
        ]

    loads, stores = pieces(sources, held, 0), pieces(held, targets, 1)
    for copy in loads:
        copy.start()
    for load, store in zip(loads, stores):
        load.wait()
        store.start()
    for copy in stores:
        copy.wait()


def settled(arrays):
    parts = min(8, arrays[0].shape[0])
    return pl.pallas_call(
        functools.partial(settle, parts),
        in_specs=[pl.BlockSpec(memory_space=pl.ANY)] * len(arrays),
        out_specs=[pl.BlockSpec(memory_space=pl.ANY)] * len(arrays),
        out_shape=[jax.ShapeDtypeStruct(a.shape, a.dtype) for a in arrays],
        scratch_shapes=[pltpu.VMEM(a.shape, a.dtype) for a in arrays]
        + [pltpu.SemaphoreType.DMA((2, parts))] * len(arrays),
    )(*arrays)


def per_device(queries, query_tangents, keys, key_tangents, values, value_tangents, span_order):
    rows, heads, head_size = queries.shape
    kv_heads = keys.shape[1]
    probes = key_tangents.shape[2]
    group = heads // kv_heads
    blks, ulys = lax.axis_size("blk"), lax.axis_size("uly")
    depth, side_x, side_y = blks // 2, 2, ulys // 2
    total_rows = rows * blks * ulys
    span_rows = total_rows // span_order.shape[0]
    tangents = query_tangents.reshape(rows, heads * probes, head_size)
    streams = jnp.concatenate(
        [
            jnp.transpose(keys, (1, 0, 2))[:, None],
            jnp.transpose(key_tangents, (1, 2, 0, 3)),
            jnp.transpose(values, (1, 0, 2))[:, None],
            jnp.transpose(value_tangents, (1, 2, 0, 3)),
        ],
        axis=1,
    )
    half = (streams.shape[1] - LAST) // 2
    packed = streams[:, : 2 * half].reshape(kv_heads, 2, half, rows, head_size)
    packed_last = streams[:, 2 * half :]
    stored = np.arange(total_rows).reshape(depth, 2, ulys, rows)
    stored = stored.transpose(1, 0, 2, 3).reshape(total_rows)
    place_table = np.stack([stored // span_rows, stored % span_rows]).astype(np.int32)
    wide_rows = rows * group * probes
    pairs = rows * heads * total_rows
    dma = pltpu.SemaphoreType.DMA
    attention, tangent = pl.pallas_call(
        functools.partial(
            exchange_and_attend, (depth, side_y, side_x), probes, group, span_rows
        ),
        in_specs=[pl.BlockSpec(memory_space=pltpu.SMEM)]
        + [pl.BlockSpec(memory_space=pl.ANY)] * 5,
        out_specs=[pl.BlockSpec(memory_space=pl.ANY)] * 2,
        out_shape=[
            jax.ShapeDtypeStruct(queries.shape, queries.dtype),
            jax.ShapeDtypeStruct(tangents.shape, tangents.dtype),
        ],
        scratch_shapes=[
            pltpu.VMEM(
                (kv_heads, 2, 2, depth, side_y, side_x, half, rows, head_size), keys.dtype
            ),
            pltpu.VMEM(
                (kv_heads, 2, depth, side_y, side_x, streams.shape[1] - 2 * half, rows, head_size),
                keys.dtype,
            ),
            pltpu.VMEM(queries.shape, queries.dtype),
            pltpu.VMEM(tangents.shape, tangents.dtype),
            pltpu.VMEM(place_table.shape, jnp.int32),
            pltpu.VMEM((rows * group, total_rows), jnp.float32),
            pltpu.VMEM((wide_rows, head_size), jnp.float32),
            pltpu.VMEM((wide_rows, head_size), jnp.float32),
            dma((5,)),
            dma((kv_heads, depth - 1)),
            dma((kv_heads, depth - 1)),
            dma((kv_heads, 4)),
            dma((kv_heads, 4)),
            dma((kv_heads, 2, side_y - 1)),
            dma((kv_heads, 2, side_y - 1)),
            dma((side_y * side_x - 1,)),
            dma((side_y * side_x - 1,)),
            dma((kv_heads, depth - 1, 2)),
            dma((kv_heads, depth - 1, 2)),
            pltpu.VMEM(queries.shape, queries.dtype),
            pltpu.VMEM(tangents.shape, tangents.dtype),
            dma((kv_heads, 2)),
        ],
        cost_estimate=pl.CostEstimate(
            flops=2 * pairs * head_size * (2 + 4 * probes),
            transcendentals=pairs,
            bytes_accessed=packed.size * 2,
        ),
        compiler_params=pltpu.CompilerParams(
            collective_id=0, has_side_effects=True, vmem_limit_bytes=67043328
        ),
    )(span_order, place_table, packed, packed_last, queries, tangents)
    attention, tangent = settled([attention, tangent])
    return attention, tangent.reshape(query_tangents.shape)


def solution(mesh):
    placed = (
        P(("blk", "uly"), None, None),
        P(("blk", "uly"), None, None, None),
        P(("blk", "uly"), None, None),
        P(("blk", "uly"), None, None, None),
        P(("blk", "uly"), None, None),
        P(("blk", "uly"), None, None, None),
        P(),
    )
    return jax.shard_map(
        per_device,
        mesh=mesh,
        in_specs=placed,
        out_specs=(P(("blk", "uly"), None, None), P(("blk", "uly"), None, None, None)),
        check_vma=False,
    )
```
